32 devices in a mesh: fsdp: 16 (over z, y, core), tp: 2 (over x).
Axes of the slice: x: 2, y: 2, z: 4, core: 2. Of those that a mesh axis runs over, the one named last changes fastest.
Arguments:
- train_x: bfloat16 [16384, 8192], P('fsdp'), may hold values from -6 to 6
- train_q: bfloat16 [16384, 8192], P('fsdp', 'tp'), may hold values from -17 to 17
- train_k: bfloat16 [16384, 1024], P('fsdp', 'tp'), may hold values from -14 to 14
- train_target: bfloat16 [16384, 8192], P('fsdp', 'tp'), may hold values from -6 to 6
- train_skill: int32 [64], replicated, may hold values from 0 to 3, as said below
- value_weight: bfloat16 [8192, 1024], P('fsdp', 'tp'), may hold values from -0.0625 to 0.0625
- val_x: bfloat16 [2048, 8192], P('fsdp'), may hold values from -6 to 6
- val_q: bfloat16 [2048, 8192], P('fsdp', 'tp'), may hold values from -17 to 17
- val_k: bfloat16 [2048, 1024], P('fsdp', 'tp'), may hold values from -14 to 14
- val_target: bfloat16 [2048, 8192], P('fsdp', 'tp'), may hold values from -6 to 6
- val_skill: int32 [16], replicated, may hold values from 0 to 3, as said below
Outputs:
- skill_grads: bfloat16 [4, 8192, 1024], P(None, 'fsdp', 'tp')
- transfer: float32 [4, 4], replicated
The draws below stay inside these ranges and needn't reach their ends.
Inputs may be any that keep to these rules, and one draw needn't show every extreme that they name: `train_skill`: each of the 4 skills labels exactly 16 sequences. `val_skill`: each of the 4 skills labels exactly 4 sequences.
All inputs are finite; a program needn't handle non-finite values.
Results may differ from the reference program's by a relative error of at most 0.0052.
The reference program's roundings to bfloat16 on the way count: a program that leaves them out, or rounds other values in their place, can miss the bound.
Values may be sent and summed in bfloat16 or wider, within the bound.
A program may use at most 256 MiB of HBM per device.

```python
import math
import jax
import jax.numpy as jnp
from jax import lax

D = 8192
HQ = 64
KVH = 8
HD = 128
SKILLS = 4
SEQ = 256
VSEQ = 128
TRAIN_SEQS = 64
VAL_SEQS = 16
TRAIN_TOKENS = 16384
VAL_TOKENS = 2048


def drawn_pair(key, rows):
    key_query, key_keys = jax.random.split(key, 2)
    queries = jax.random.truncated_normal(key_query, -4.0, 4.0, (rows, HQ * HD), jnp.float32)
    keys = jax.random.truncated_normal(key_keys, -4.0, 4.0, (rows, KVH * HD), jnp.float32)
    return (queries, keys)


def draw_train_q(key, part):
    return drawn_pair(jax.random.fold_in(key, 31), TRAIN_TOKENS)[0].astype(jnp.bfloat16)


def draw_train_k(key, part):
    return drawn_pair(jax.random.fold_in(key, 31), TRAIN_TOKENS)[1].astype(jnp.bfloat16)


def draw_val_q(key, part):
    return drawn_pair(jax.random.fold_in(key, 47), VAL_TOKENS)[0].astype(jnp.bfloat16)


def draw_val_k(key, part):
    return drawn_pair(jax.random.fold_in(key, 47), VAL_TOKENS)[1].astype(jnp.bfloat16)


def draw_train_skill(key, part):
    shuffled = jax.random.permutation(jax.random.fold_in(key, 5), TRAIN_SEQS)
    return (shuffled % SKILLS).astype(jnp.int32)


def draw_val_skill(key, part):
    shuffled = jax.random.permutation(jax.random.fold_in(key, 9), VAL_SEQS)
    return (shuffled % SKILLS).astype(jnp.int32)


def strengthened(entries, own_key, source, target, shards_of, factor):
    owner, partner = [(jnp.arange(entries.shape[position]) // (entries.shape[position] // shards_of)).reshape([-1 if axis == position else 1 for axis in range(entries.ndim)]) for position in (source, target)]
    chosen = jax.random.permutation(own_key, shards_of)[partner]
    strong = (owner == chosen) | (owner == (partner + shards_of // 2) % shards_of)
    return jnp.where(strong, factor * entries, entries)


def block_scale(key, dims, shards, smallest, top_value):
    loudness, own = 1.0, jax.random.fold_in(key, 6)
    for position, parts in shards:
        steps = jnp.exp(jax.random.uniform(jax.random.fold_in(own, position), (parts,), jnp.float32, smallest / len(shards), top_value / len(shards)))
        loudness = loudness * jnp.repeat(steps, dims[position] // parts).reshape([-1 if axis == position else 1 for axis in range(len(dims))])
    return loudness


def bell_draw(key, extent, scale, most, shards=(), kind=jnp.bfloat16):
    values = jax.random.normal(key, extent, jnp.float32) * scale
    if len(shards) > 0:
        values = block_scale(key, extent, shards, -0.22, 0.18) * values
    return jnp.clip(values, min=-most, max=most).astype(kind)


def bell_draw_with(own_key, dims, width, limit, cuts, heavy, kind=jnp.bfloat16):
    values = width * jax.random.normal(own_key, dims, jnp.float32)
    if cuts:
        values = values * block_scale(own_key, dims, cuts, -0.22, 0.18)
    return jnp.clip(strengthened(values, jax.random.fold_in(own_key, 3), *heavy), -limit, limit).astype(kind)


def setup_inputs(seed: int = 0) -> dict:
    key_of = jax.random.split(jax.random.key(seed), 12)
    train_x = bell_draw_with(key_of[0], (TRAIN_TOKENS, D), 1.0, 6.0, ((0, 16),), (0, 1, 16, 2.0))
    train_q = draw_train_q(jax.random.fold_in(key_of[11], 71), 0)
    train_k = draw_train_k(jax.random.fold_in(key_of[11], 71), 0)
    train_target = bell_draw(key_of[3], (TRAIN_TOKENS, HQ * HD), 1.0, 6.0, ((0, 16), (1, 2)))
    train_skill = draw_train_skill(jax.random.fold_in(key_of[11], 71), 0)
    value_weight = bell_draw(key_of[5], (D, KVH * HD), D ** -0.5, 0.0625, ((0, 16), (1, 2)))
    val_x = bell_draw(key_of[6], (VAL_TOKENS, D), 1.0, 6.0, ((0, 16),))
    val_q = draw_val_q(jax.random.fold_in(key_of[11], 71), 0)
    val_k = draw_val_k(jax.random.fold_in(key_of[11], 71), 0)
    val_target = bell_draw(key_of[9], (VAL_TOKENS, HQ * HD), 1.0, 6.0, ((0, 16), (1, 2)))
    val_skill = draw_val_skill(jax.random.fold_in(key_of[11], 71), 0)
    return {"train_x": train_x, "train_q": train_q, "train_k": train_k, "train_target": train_target, "train_skill": train_skill, "value_weight": value_weight, "val_x": val_x, "val_q": val_q, "val_k": val_k, "val_target": val_target, "val_skill": val_skill}


step_size = 0.01

def attend(query_rows, key_rows, length):
    kv_heads = key_rows.shape[1] // HD
    group = query_rows.shape[1] // HD // kv_heads
    queries = query_rows.reshape(length, kv_heads, group, HD).astype(jnp.float32)
    keys = key_rows.reshape(length, kv_heads, HD).astype(jnp.float32)
    scores = jnp.einsum('qgrh,kgh->grqk', queries, keys) * (1.0 / math.sqrt(HD))
    places = jnp.arange(length)
    allowed = places[:, None] >= places[None, :]
    scores = jnp.where(allowed, scores, jnp.float32(-1e+30))
    highest = lax.optimization_barrier(jnp.max(scores, axis=-1, keepdims=True))
    raised = jnp.exp(scores - highest)
    return (raised / lax.optimization_barrier(jnp.sum(raised, axis=-1, keepdims=True))).astype(jnp.bfloat16)

def mix_heads(attention, value_rows, length):
    kv_heads = attention.shape[0]
    blocks = value_rows.reshape(length, kv_heads, HD).astype(jnp.float32)
    mixed = jnp.einsum('grqk,kgh->qgrh', attention.astype(jnp.float32), blocks)
    return mixed

def reference(train_x, train_q, train_k, train_target, train_skill, value_weight, val_x, val_q, val_k, val_target, val_skill):
    head_width = value_weight.shape[1]
    values = jnp.dot(train_x, value_weight, preferred_element_type=jnp.float32).astype(jnp.bfloat16)
    val_values = jnp.dot(val_x, value_weight, preferred_element_type=jnp.float32).astype(jnp.bfloat16)

    def train_sequence(inputs):
        query_rows, key_rows, value_rows, target_rows = inputs
        attention = attend(query_rows, key_rows, SEQ)
        mixed = mix_heads(attention, value_rows, SEQ)
        target_blocks = target_rows.reshape(mixed.shape).astype(jnp.float32)
        residual = ((mixed - target_blocks) / SEQ).astype(jnp.bfloat16)
        pulled = jnp.einsum('grqk,qgrh->kgh', attention.astype(jnp.float32), residual.astype(jnp.float32))
        return pulled.reshape(SEQ, head_width).astype(jnp.bfloat16)
    value_grads = lax.map(train_sequence, (train_q.reshape(TRAIN_SEQS, SEQ, -1), train_k.reshape(TRAIN_SEQS, SEQ, -1), values.reshape(TRAIN_SEQS, SEQ, -1), train_target.reshape(TRAIN_SEQS, SEQ, -1)))
    order = jnp.argsort(train_skill, stable=True).astype(jnp.int32)
    per_skill = TRAIN_SEQS // SKILLS
    chosen = order.reshape(SKILLS, per_skill)
    input_seqs = train_x.reshape(TRAIN_SEQS, SEQ, D)

    def skill_gradient(rows):
        inputs_here = input_seqs[rows].reshape(per_skill * SEQ, D)
        grads_here = value_grads[rows].reshape(per_skill * SEQ, head_width)
        return jnp.dot(inputs_here.T, grads_here, preferred_element_type=jnp.float32).astype(jnp.bfloat16)
    skill_grads = lax.map(skill_gradient, chosen)

    def val_sequence(inputs):
        query_rows, key_rows, value_rows, target_rows = inputs
        attention = attend(query_rows, key_rows, VSEQ)
        mixed = mix_heads(attention, value_rows, VSEQ)
        target_blocks = target_rows.reshape(mixed.shape).astype(jnp.float32)
        val_residual = (mixed - target_blocks) / VSEQ
        pulled = jnp.einsum('grqk,qgrh->kgh', attention.astype(jnp.float32), val_residual, precision=lax.Precision.HIGHEST)
        return pulled.reshape(VSEQ, head_width)
    val_pull = lax.map(val_sequence, (val_q.reshape(VAL_SEQS, VSEQ, -1), val_k.reshape(VAL_SEQS, VSEQ, -1), val_values.reshape(VAL_SEQS, VSEQ, -1), val_target.reshape(VAL_SEQS, VSEQ, -1))).reshape(VAL_TOKENS, head_width)
    stacked = jnp.transpose(skill_grads, (1, 0, 2)).reshape(D, SKILLS * head_width)
    tangent = jnp.dot(val_x, stacked, preferred_element_type=jnp.float32).reshape(VAL_TOKENS, SKILLS, head_width)
    along = jnp.einsum('tsc,tc->ts', tangent, val_pull, precision=lax.Precision.HIGHEST)
    token_skill = jnp.repeat(val_skill, VSEQ)
    indicator = (token_skill[:, None] == jnp.arange(SKILLS, dtype=jnp.int32)[None, :]).astype(jnp.float32)
    transfer = step_size * jnp.dot(along.T, indicator, precision=lax.Precision.HIGHEST)
    return (skill_grads, transfer)
```

```python
import functools
import math

import jax
import jax.numpy as jnp
from jax import lax
from jax.experimental import pallas as pl
from jax.experimental.pallas import tpu as pltpu
from jax.sharding import PartitionSpec as P

HD = 128
SKILLS = 4
SEQ = 256
VSEQ = 128


step_size = 0.01


def attend(query_rows, key_rows, length):
    members = query_rows.shape[0] // length
    kv_heads = key_rows.shape[1] // HD
    group = query_rows.shape[1] // HD // kv_heads
    queries = query_rows.reshape(members, length, kv_heads, group, HD)
    keys = key_rows.reshape(members, length, kv_heads, HD)
    scores = jnp.einsum("bqgrh,bkgh->bgrqk", queries, keys, preferred_element_type=jnp.float32) * (
        1.0 / math.sqrt(HD)
    )
    places = jnp.arange(length)
    allowed = places[:, None] >= places[None, :]
    scores = jnp.where(allowed, scores, jnp.float32(-1e30))
    highest = jnp.max(scores, axis=-1, keepdims=True)
    raised = jnp.exp(scores - highest)
    return (raised / jnp.sum(raised, axis=-1, keepdims=True)).astype(jnp.bfloat16)


def grad_kernel(group, length, q_ref, k_ref, v_ref, t_ref, o_ref):
    keys = k_ref[...]
    vals = v_ref[...]
    key_at = lax.broadcasted_iota(jnp.int32, (length, length), 0)
    query_at = lax.broadcasted_iota(jnp.int32, (length, length), 1)
    allowed = query_at >= key_at
    total = jnp.zeros((length, HD), jnp.float32)
    for h in range(group):
        cols = slice(h * HD, (h + 1) * HD)
        scores = lax.dot_general(
            keys, q_ref[:, cols], (((1,), (1,)), ((), ())), preferred_element_type=jnp.float32
        ) * (1.0 / math.sqrt(HD))
        scores = jnp.where(allowed, scores, jnp.float32(-1e30))
        raised = jnp.exp(scores - jnp.max(scores, axis=0, keepdims=True))
        share = 1.0 / jnp.sum(raised, axis=0, keepdims=True)
        attention = (raised * share).astype(jnp.bfloat16)
        mixed = lax.dot_general(
            attention, vals, (((0,), (0,)), ((), ())), preferred_element_type=jnp.float32
        )
        residual = ((mixed - t_ref[:, cols].astype(jnp.float32)) * (1.0 / length)).astype(jnp.bfloat16)
        total += jnp.dot(attention, residual, preferred_element_type=jnp.float32)
    o_ref[...] = total.astype(o_ref.dtype)


def sequence_grads(q, k, v, target, length):
    rows, width = k.shape
    heads = width // HD
    group = q.shape[1] // width
    wide = pl.BlockSpec((length, group * HD), lambda b, g: (b, g))
    narrow = pl.BlockSpec((length, HD), lambda b, g: (b, g))
    return pl.pallas_call(
        functools.partial(grad_kernel, group, length),
        grid=(rows // length, heads),
        in_specs=[wide, narrow, narrow, wide],
        out_specs=narrow,
        out_shape=jax.ShapeDtypeStruct((rows, width), jnp.bfloat16),
        compiler_params=pltpu.CompilerParams(dimension_semantics=("arbitrary", "arbitrary")),
        cost_estimate=pl.CostEstimate(
            flops=6 * rows * length * width * group,
            bytes_accessed=4 * rows * width * (group + 1),
            transcendentals=rows * length * heads * group,
        ),
    )(q, k, v, target)


def skill_kernel(parts, spare, info_ref, *refs):
    xs, gs, o_ref, acc = refs[:parts], refs[parts : 2 * parts], refs[2 * parts], refs[2 * parts + 1]
    step = pl.program_id(0)

    @pl.when(step == 0)
    def _():
        acc[...] = jnp.zeros_like(acc)

    for o in range(parts):
        slot = info_ref[spare + step * parts + o]
        acc[slot] += lax.dot_general(
            xs[o][...], gs[o][...], (((0,), (0,)), ((), ())), preferred_element_type=jnp.float32
        )

    @pl.when(step == pl.num_programs(0) - 1)
    def _():
        o_ref[...] = acc[...].astype(o_ref.dtype)


def skill_products(xs, gs, g_block, info, spare, length, out_dtype):
    parts = len(xs)
    rows, width = xs[0].shape[1], gs[0].shape[1]
    steps = xs[0].shape[0] // length
    in_specs = [pl.BlockSpec((length, rows), lambda i, info: (i, 0)) for _ in range(parts)]
    in_specs += [
        pl.BlockSpec((length, width), functools.partial(lambda o, i, info: (g_block(o, i, info), 0), o))
        for o in range(parts)
    ]
    return pl.pallas_call(
        functools.partial(skill_kernel, parts, spare),
        grid_spec=pltpu.PrefetchScalarGridSpec(
            num_scalar_prefetch=1,
            grid=(steps,),
            in_specs=in_specs,
            out_specs=pl.BlockSpec((SKILLS, rows, width), lambda i, info: (0, 0, 0)),
            scratch_shapes=[pltpu.VMEM((SKILLS, rows, width), jnp.float32)],
        ),
        out_shape=jax.ShapeDtypeStruct((SKILLS, rows, width), out_dtype),
        compiler_params=pltpu.CompilerParams(dimension_semantics=("arbitrary",)),
        cost_estimate=pl.CostEstimate(
            flops=2 * parts * xs[0].shape[0] * rows * width,
            bytes_accessed=2 * parts * xs[0].shape[0] * (rows + width),
            transcendentals=0,
        ),
    )(info, *xs, *gs)


def transfer_matrix(
    train_x,
    train_q,
    train_k,
    train_target,
    train_skill,
    value_weight,
    val_x,
    val_q,
    val_k,
    val_target,
    val_skill,
):
    shards = lax.axis_size("fsdp")
    splits = lax.axis_size("tp")
    turn = lax.axis_index("tp")
    head_width = train_k.shape[1]
    kv_heads = head_width // HD
    group = train_q.shape[1] // head_width
    train_rows, depth = train_x.shape
    val_rows = val_x.shape[0]
    train_members = train_rows // SEQ
    val_members = val_rows // VSEQ
    rows_own = depth // shards

    shard_rows = lax.all_gather(value_weight, "fsdp", axis=0, tiled=True)

    if train_members % splits:
        splits, turn = 1, 0
    share = train_members // splits
    held = train_x.reshape(splits, share, SEQ, shards, rows_own)
    held = lax.dynamic_index_in_dim(held, turn, axis=0, keepdims=False)
    x_parts = []
    for piece in range(share):
        blocks = held[piece].transpose(1, 0, 2)
        own = lax.all_to_all(blocks, "fsdp", split_axis=0, concat_axis=0, tiled=True)
        own = own.reshape(shards * SEQ, rows_own)
        x_parts += [own] + [
            lax.ppermute(own, "tp", [(i, (i + o) % splits) for i in range(splits)]) for o in range(1, splits)
        ]
    val_blocks_x = val_x.reshape(val_rows, shards, rows_own).transpose(1, 0, 2)
    val_cols = lax.all_to_all(val_blocks_x, "fsdp", split_axis=0, concat_axis=0, tiled=True)
    val_cols = val_cols.reshape(shards * val_rows, rows_own)

    val_values = jnp.dot(val_x, shard_rows, preferred_element_type=jnp.float32).astype(jnp.bfloat16)
    values = jnp.dot(train_x, shard_rows, preferred_element_type=jnp.float32).astype(jnp.bfloat16)

    grad_rows = sequence_grads(train_q, train_k, values, train_target, SEQ)
    all_grads = lax.all_gather(grad_rows, "fsdp", axis=0, tiled=True)

    val_attention = attend(val_q, val_k, VSEQ)
    val_blocks = val_values.reshape(val_members, VSEQ, kv_heads, HD)
    val_mixed = jnp.einsum(
        "bgrqk,bkgh->bqgrh", val_attention, val_blocks, preferred_element_type=jnp.float32
    )
    val_target_blocks = val_target.reshape(val_members, VSEQ, kv_heads, group, HD).astype(
        jnp.float32
    )
    val_residual = (val_mixed - val_target_blocks) / VSEQ
    val_pull = jnp.einsum(
        "bgrqk,bqgrh->bkgh",
        val_attention.astype(jnp.float32),
        val_residual,
        precision=lax.Precision.HIGHEST,
    )
    val_pull = val_pull.reshape(val_rows, head_width)
    pulls = lax.all_gather(val_pull, "fsdp", axis=0, tiled=True)
    coarse = lax.reduce_precision(pulls, 8, 7)
    fine = (pulls - coarse).astype(jnp.bfloat16)
    coarse = coarse.astype(jnp.bfloat16)
    val_products = skill_products(
        [val_cols, val_cols],
        [coarse, fine],
        lambda o, i, info: i,
        jnp.repeat(val_skill, 2),
        0,
        VSEQ,
        jnp.float32,
    )

    owner = jnp.arange(shards, dtype=jnp.int32)
    places = [
        owner * train_members + lax.rem(turn - o + splits, splits) * share + piece
        for piece in range(share)
        for o in range(splits)
    ]
    places = jnp.stack(places, axis=1)
    chosen = places[:, :, None] == jnp.arange(train_skill.shape[0], dtype=jnp.int32)
    skills_there = jnp.sum(jnp.where(chosen, train_skill, 0), axis=-1)
    info = jnp.concatenate([places.reshape(-1), skills_there.reshape(-1)]).astype(jnp.int32)
    skill_grads = skill_products(
        x_parts,
        [all_grads] * train_members,
        lambda o, i, info: info[i * train_members + o],
        info,
        places.size,
        SEQ,
        jnp.bfloat16,
    )
    transfer = step_size * jnp.sum(
        skill_grads.astype(jnp.float32)[:, None] * val_products[None, :], axis=(2, 3)
    )
    for axis in ("fsdp", "tp"):
        count = lax.axis_size(axis)
        reach = 1
        while reach < count:
            transfer = transfer + lax.ppermute(transfer, axis, [(i, i ^ reach) for i in range(count)])
            reach *= 2
    return (skill_grads, transfer)


def solution(mesh):
    placed = (
        P("fsdp", None),
        P("fsdp", "tp"),
        P("fsdp", "tp"),
        P("fsdp", "tp"),
        P(),
        P("fsdp", "tp"),
        P("fsdp", None),
        P("fsdp", "tp"),
        P("fsdp", "tp"),
        P("fsdp", "tp"),
        P(),
    )
    return jax.shard_map(
        transfer_matrix,
        mesh=mesh,
        in_specs=placed,
        out_specs=(P(None, "fsdp", "tp"), P()),
        check_vma=False,
    )
```
